32 devices in a mesh: replica: 8 (over z, y), shard: 4 (over x, core).
Axes of the slice: x: 2, y: 2, z: 4, core: 2. Of those that a mesh axis runs over, the one named last changes fastest.
Arguments:
- tokens: bfloat16 [16, 256, 1152], P('replica', 'shard'), may hold values from -6 to 6
- positions: int32 [16, 256], P('replica', 'shard'), may hold values from 0 to 255, as said below
- cotangent: bfloat16 [16, 256, 1152], P('replica', 'shard'), may hold values from -6 to 6
- live_count: int32 [8], P('replica'), may hold values from 1 to 2, as said below
- qkv_weight: bfloat16 [1152, 1536], P('shard'), may hold values from -0.1875 to 0.1875
- out_weight: bfloat16 [1024, 1152], P('shard'), may hold values from -0.1875 to 0.1875
- gate_weight: bfloat16 [1152, 6912], P('shard'), may hold values from -0.1875 to 0.1875
- up_weight: bfloat16 [1152, 6912], P('shard'), may hold values from -0.1875 to 0.1875
- down_weight: bfloat16 [6912, 1152], P('shard'), may hold values from -0.078125 to 0.078125
- gain_in: float32 [1152], replicated, may hold values from 0.25 to 1.75
- gain_query: float32 [256], replicated, may hold values from 0.25 to 1.75
- gain_key: float32 [256], replicated, may hold values from 0.25 to 1.75
- gain_attn: float32 [1152], replicated, may hold values from 0.25 to 1.75
- gain_pre: float32 [1152], replicated, may hold values from 0.25 to 1.75
- gain_post: float32 [1152], replicated, may hold values from 0.25 to 1.75
Outputs:
- output: float32 [16, 256, 1152], P('replica', 'shard')
- input_grad: float32 [16, 256, 1152], P('replica', 'shard')
- qkv_grad: float32 [1152, 1536], P('shard', 'replica')
- out_grad: float32 [1024, 1152], P('shard', 'replica')
- gate_grad: float32 [1152, 6912], P('shard', 'replica')
- up_grad: float32 [1152, 6912], P('shard', 'replica')
- down_grad: float32 [6912, 1152], P('shard', 'replica')
- gain_in_grad: float32 [1152], replicated
- gain_query_grad: float32 [256], replicated
- gain_key_grad: float32 [256], replicated
- gain_attn_grad: float32 [1152], replicated
- gain_pre_grad: float32 [1152], replicated
- gain_post_grad: float32 [1152], replicated
The draws below stay inside these ranges and needn't reach their ends.
Inputs may be any that keep to these rules, and one draw needn't show every extreme that they name: Each sequence holds one or two documents whose positions count from 0 by one; some sequence is a single document of 256 tokens. `live_count`: some group has all 2 slots live.
All inputs are finite; a program needn't handle non-finite values.
Results may differ from the reference program's by a relative error of at most 0.015.
Values may be sent and summed in bfloat16 or wider, within the bound.
No kernel may reach another device: no remote copies, remote signals or barrier semaphores. Data moves between devices by JAX's collectives and lax.ppermute only.
A program may use at most 192 MiB of HBM per device.

```python
import math
import jax
import jax.numpy as jnp
from jax import lax

D = 1152
H = 4
HD = 256
FF = 6912
LEN = 256
SLOTS = 2
GROUPS = 8
NSEQ = 16


def draw_positions(key, part):
    cuts = jax.random.randint(key, (NSEQ, 1), 0, LEN)
    cuts = cuts.at[0, 0].set(0)
    seq_index = jnp.arange(LEN, dtype=jnp.int32)[None, :]
    return jnp.where(seq_index >= cuts, seq_index - cuts, seq_index).astype(jnp.int32)


def draw_live_count(key, part):
    counts = jax.random.randint(key, (GROUPS,), 1, SLOTS + 1)
    full_group = jax.random.randint(jax.random.fold_in(key, 7), (), 0, GROUPS)
    return jnp.where(jnp.arange(GROUPS) == full_group, SLOTS, counts).astype(jnp.int32)


def block_levels(stream_key, extent, shards, smallest, top_value):
    factor_of, own = 1.0, jax.random.fold_in(stream_key, 6)
    for dim, blocks in shards:
        heights = jnp.exp(jax.random.uniform(jax.random.fold_in(own, dim), (blocks,), jnp.float32, smallest / len(shards), top_value / len(shards)))
        factor_of = factor_of * jnp.repeat(heights, extent[dim] // blocks).reshape([-1 if axis == dim else 1 for axis in range(len(extent))])
    return factor_of


def gaussian(stream_key, dims, spread, most, shards=(), kind=jnp.bfloat16):
    entries = spread * jax.random.normal(stream_key, dims, jnp.float32)
    if shards:
        entries = entries * block_levels(stream_key, dims, shards, -0.22, 0.18)
    return jnp.clip(entries, -most, most).astype(kind)


def setup_inputs(seed: int = 0) -> dict:
    streams_of = jax.random.split(jax.random.key(seed), 16)
    tokens = gaussian(streams_of[0], (NSEQ, LEN, D), 1.0, 6.0, ((0, 8), (1, 4)))
    positions = draw_positions(jax.random.fold_in(streams_of[15], 71), 0)
    cotangent = gaussian(streams_of[2], (NSEQ, LEN, D), 1.0, 6.0, ((0, 8), (1, 4)))
    live_count = draw_live_count(jax.random.fold_in(streams_of[15], 71), 0)
    qkv_weight = gaussian(streams_of[4], (D, (H + 2) * HD), D ** -0.5, 0.1875, ((0, 4),))
    out_weight = gaussian(streams_of[5], (H * HD, D), (H * HD) ** -0.5, 0.1875, ((0, 4),))
    gate_weight = gaussian(streams_of[6], (D, FF), D ** -0.5, 0.1875, ((0, 4),))
    up_weight = gaussian(streams_of[7], (D, FF), D ** -0.5, 0.1875, ((0, 4),))
    down_weight = gaussian(streams_of[8], (FF, D), FF ** -0.5, 0.078125, ((0, 4),))
    gain_in = jnp.clip(1.0 + 0.15 * jax.random.normal(streams_of[9], (D,), jnp.float32), 0.25, 1.75)
    gain_query = jnp.clip(1.0 + 0.15 * jax.random.normal(streams_of[10], (HD,), jnp.float32), 0.25, 1.75)
    gain_key = jnp.clip(1.0 + 0.15 * jax.random.normal(streams_of[11], (HD,), jnp.float32), 0.25, 1.75)
    gain_attn = jnp.clip(1.0 + 0.15 * jax.random.normal(streams_of[12], (D,), jnp.float32), 0.25, 1.75)
    gain_pre = jnp.clip(1.0 + 0.15 * jax.random.normal(streams_of[13], (D,), jnp.float32), 0.25, 1.75)
    gain_post = jnp.clip(1.0 + 0.15 * jax.random.normal(streams_of[14], (D,), jnp.float32), 0.25, 1.75)
    return dict(tokens=tokens, positions=positions, cotangent=cotangent, live_count=live_count, qkv_weight=qkv_weight, out_weight=out_weight, gate_weight=gate_weight, up_weight=up_weight, down_weight=down_weight, gain_in=gain_in, gain_query=gain_query, gain_key=gain_key, gain_attn=gain_attn, gain_pre=gain_pre, gain_post=gain_post)


epsilon = 1e-06
rope_base = 1000000.0
score_scale = 0.0625
masked_score = -1e+30

def rms_norm(values, gain_vec):
    inv_rms = lax.rsqrt(lax.optimization_barrier(jnp.mean(values * values, axis=-1, keepdims=True)) + epsilon)
    return values * inv_rms * gain_vec

def norm_back(values, gain_vec, upstream):
    inv_rms = lax.rsqrt(lax.optimization_barrier(jnp.mean(values * values, axis=-1, keepdims=True)) + epsilon)
    unit_val = values * inv_rms
    gain_grad = lax.optimization_barrier(jnp.sum((upstream * unit_val).reshape(-1, values.shape[-1]), axis=0))
    inner_grad = upstream * gain_vec
    value_grad = inv_rms * (inner_grad - unit_val * lax.optimization_barrier(jnp.mean(inner_grad * unit_val, axis=-1, keepdims=True)))
    return (value_grad, gain_grad)

def rotary(pos_rows):
    half_dim = HD // 2
    frequency = rope_base ** (-(jnp.arange(half_dim, dtype=jnp.float32) * 2.0 / HD))
    angles = pos_rows.astype(jnp.float32)[:, None] * frequency[None, :]
    angles = jnp.concatenate([angles, angles], axis=1)
    return (jnp.cos(angles), jnp.sin(angles))

def rotate(values, cosine, sine):
    half_dim = values.shape[-1] // 2
    lower_half = values[..., :half_dim]
    upper_half = values[..., half_dim:]
    turned = jnp.concatenate([-upper_half, lower_half], axis=-1)
    return values * cosine + turned * sine

def gelu_tanh(values):
    return jax.nn.gelu(values, approximate=True)

def dot32(left, right):
    return jnp.dot(left, right, preferred_element_type=jnp.float32)

def layer(tokens, positions, cotangent, live_seq, qkv_weight, out_weight, gate_weight, up_weight, down_weight, gain_in, gain_query, gain_key, gain_attn, gain_pre, gain_post):
    seq_count, seq_len, model_width = tokens.shape
    token_rows = seq_count * seq_len
    inner_width = H * HD
    seq_index = jnp.arange(seq_len, dtype=jnp.int32)
    causal = seq_index[:, None] >= seq_index[None, :]
    inputs = tokens.reshape(token_rows, model_width).astype(jnp.float32)
    normed_in = rms_norm(inputs, gain_in).astype(jnp.bfloat16)
    projected = dot32(normed_in, qkv_weight)
    cosine, sine = rotary(positions.reshape(token_rows))
    query_pre = projected[:, :inner_width].reshape(token_rows, H, HD)
    key_pre = projected[:, inner_width:inner_width + HD]
    queries = rotate(rms_norm(query_pre, gain_query), cosine[:, None], sine[:, None]).astype(jnp.bfloat16)
    key_rows = rotate(rms_norm(key_pre, gain_key), cosine, sine).astype(jnp.bfloat16)
    value_rows = projected[:, inner_width + HD:].astype(jnp.bfloat16)
    query_blocks = queries.reshape(seq_count, seq_len, H, HD).astype(jnp.float32)
    key_blocks = key_rows.reshape(seq_count, seq_len, HD).astype(jnp.float32)
    value_blocks = value_rows.reshape(seq_count, seq_len, HD).astype(jnp.float32)
    raw_scores = jnp.einsum('sqhd,skd->shqk', query_blocks, key_blocks) * score_scale
    raw_scores = jnp.where(causal[None, None], raw_scores, masked_score)
    row_max = lax.optimization_barrier(jnp.max(raw_scores, axis=-1, keepdims=True))
    log_total = row_max + jnp.log(lax.optimization_barrier(jnp.sum(jnp.exp(raw_scores - row_max), axis=-1, keepdims=True)))
    probs = jnp.exp(raw_scores - log_total)
    probs_bf = probs.astype(jnp.bfloat16)
    mixed = jnp.einsum('shqk,skd->sqhd', probs_bf.astype(jnp.float32), value_blocks)
    mixed_bf = mixed.reshape(token_rows, inner_width).astype(jnp.bfloat16)
    attended = dot32(mixed_bf, out_weight)
    residual = inputs + rms_norm(attended, gain_attn)
    normed_pre = rms_norm(residual, gain_pre).astype(jnp.bfloat16)
    gate_pre = dot32(normed_pre, gate_weight)
    up_pre = dot32(normed_pre, up_weight)
    activated, gelu_back = jax.vjp(gelu_tanh, gate_pre)
    hidden = (activated * up_pre).astype(jnp.bfloat16)
    ffn_out = dot32(hidden, down_weight)
    output = residual + rms_norm(ffn_out, gain_post)
    live_rows = jnp.repeat(live_seq, seq_len)[:, None]
    upstream = cotangent.reshape(token_rows, model_width).astype(jnp.float32) * live_rows
    ffn_grad, post_grad = norm_back(ffn_out, gain_post, upstream)
    ffn_grad_bf = ffn_grad.astype(jnp.bfloat16)
    hidden_grad = dot32(ffn_grad_bf, down_weight.T)
    down_term = dot32(hidden.T, ffn_grad_bf)
    gate_grad_bf = gelu_back(hidden_grad * up_pre)[0].astype(jnp.bfloat16)
    up_grad_bf = (hidden_grad * activated).astype(jnp.bfloat16)
    gate_term = dot32(normed_pre.T, gate_grad_bf)
    up_term = dot32(normed_pre.T, up_grad_bf)
    pre_in_grad = dot32(gate_grad_bf, gate_weight.T) + dot32(up_grad_bf, up_weight.T)
    res_part, pre_grad = norm_back(residual, gain_pre, pre_in_grad)
    residual_grad = upstream + res_part
    attn_out_grad, attn_grad = norm_back(attended, gain_attn, residual_grad)
    attn_out_bf = attn_out_grad.astype(jnp.bfloat16)
    out_term = dot32(mixed_bf.T, attn_out_bf)
    mixed_grad = dot32(attn_out_bf, out_weight.T).astype(jnp.bfloat16)
    mixed_grad = mixed_grad.reshape(seq_count, seq_len, H, HD).astype(jnp.float32)
    prob_grad = jnp.einsum('sqhd,skd->shqk', mixed_grad, value_blocks)
    row_dot = lax.optimization_barrier(jnp.sum(probs * prob_grad, axis=-1, keepdims=True))
    score_grad = (probs * (prob_grad - row_dot) * score_scale).astype(jnp.bfloat16).astype(jnp.float32)
    value_grad = jnp.einsum('shqk,sqhd->skd', probs_bf.astype(jnp.float32), mixed_grad)
    query_grad = jnp.einsum('shqk,skd->sqhd', score_grad, key_blocks)
    key_grad = jnp.einsum('shqk,sqhd->skd', score_grad, query_blocks)
    query_unrot = rotate(query_grad.reshape(token_rows, H, HD), cosine[:, None], -sine[:, None])
    query_in, query_gain_grad = norm_back(query_pre, gain_query, query_unrot)
    key_unrot = rotate(key_grad.reshape(token_rows, HD), cosine, -sine)
    key_in, key_gain_grad = norm_back(key_pre, gain_key, key_unrot)
    packed_grad = jnp.concatenate([query_in.reshape(token_rows, inner_width), key_in, value_grad.reshape(token_rows, HD)], axis=1).astype(jnp.bfloat16)
    qkv_term = dot32(normed_in.T, packed_grad)
    normed_grad = dot32(packed_grad, qkv_weight.T)
    input_part, in_grad = norm_back(inputs, gain_in, normed_grad)
    input_grad = residual_grad + input_part
    terms = (qkv_term, out_term, gate_term, up_term, down_term)
    gain_terms = (in_grad, query_gain_grad, key_gain_grad, attn_grad, pre_grad, post_grad)
    return (output.reshape(seq_count, seq_len, model_width), input_grad.reshape(seq_count, seq_len, model_width), terms, gain_terms)

def reference(tokens, positions, cotangent, live_count, qkv_weight, out_weight, gate_weight, up_weight, down_weight, gain_in, gain_query, gain_key, gain_attn, gain_pre, gain_post):
    seq_total = tokens.shape[0]
    group_size = math.gcd(seq_total, 16)
    block_count = seq_total // group_size
    seq_ids = jnp.arange(seq_total, dtype=jnp.int32)
    live_seq = (seq_ids % SLOTS < live_count[seq_ids // SLOTS]).astype(jnp.float32)
    blocks = (tokens.reshape(block_count, group_size, LEN, D), positions.reshape(block_count, group_size, LEN), cotangent.reshape(block_count, group_size, LEN, D), live_seq.reshape(block_count, group_size))
    weights = (qkv_weight, out_weight, gate_weight, up_weight, down_weight)
    gains = (gain_in, gain_query, gain_key, gain_attn, gain_pre, gain_post)
    start = (tuple((jnp.zeros(w.shape, jnp.float32) for w in weights)), tuple((jnp.zeros(g.shape, jnp.float32) for g in gains)))

    def step(carry, block_in):
        output, input_grad, terms, gain_terms = layer(block_in[0], block_in[1], block_in[2], block_in[3], qkv_weight, out_weight, gate_weight, up_weight, down_weight, gain_in, gain_query, gain_key, gain_attn, gain_pre, gain_post)
        carry = jax.tree.map(lambda left, right: left + right, carry, (terms, gain_terms))
        return (carry, (output, input_grad))
    (terms, gain_terms), (outputs, input_grads) = lax.scan(step, start, blocks)
    output = outputs.reshape(seq_total, LEN, D)
    input_grad = input_grads.reshape(seq_total, LEN, D)
    return (output, input_grad, terms[0], terms[1], terms[2], terms[3], terms[4], gain_terms[0], gain_terms[1], gain_terms[2], gain_terms[3], gain_terms[4], gain_terms[5])
```

```python
import jax
import jax.numpy as jnp
from jax import lax
from jax.experimental import pallas as pl
from jax.experimental.layout import Layout, with_layout_constraint
from jax.experimental.pallas import tpu as pltpu
from jax.sharding import PartitionSpec as P

H = 4
HD = 256


epsilon = 1e-06
rope_base = 1000000.0
score_scale = 0.0625
masked_score = -1e30
f32 = jnp.float32
bf16 = jnp.bfloat16

BLOCKS = (0, 2, 1, 3)


def rms_norm(values, gain_vec):
    inv_rms = lax.rsqrt(jnp.mean(values * values, axis=-1, keepdims=True) + epsilon)
    return values * inv_rms * gain_vec


def norm_back(values, gain_vec, upstream):
    inv_rms = lax.rsqrt(jnp.mean(values * values, axis=-1, keepdims=True) + epsilon)
    unit_val = values * inv_rms
    gain_grad = jnp.sum((upstream * unit_val).reshape(-1, values.shape[-1]), axis=0)
    inner_grad = upstream * gain_vec
    value_grad = inv_rms * (
        inner_grad - unit_val * jnp.mean(inner_grad * unit_val, axis=-1, keepdims=True)
    )
    return (value_grad, gain_grad)


def rotary(pos_rows):
    half_dim = HD // 2
    frequency = rope_base ** (-(jnp.arange(half_dim, dtype=f32) * 2.0 / HD))
    angles = pos_rows[:, None] * frequency[None, :]
    cosine, sine = jnp.cos(angles), jnp.sin(angles)
    return (jnp.concatenate([cosine, cosine], axis=1), jnp.concatenate([sine, sine], axis=1))


def rotate(values, cosine, sine):
    half_dim = values.shape[-1] // 2
    lower_half = values[..., :half_dim]
    upper_half = values[..., half_dim:]
    turned = jnp.concatenate([-upper_half, lower_half], axis=-1)
    return values * cosine + turned * sine


def gelu_tanh(values):
    return jax.nn.gelu(values, approximate=True)


def dot(spec, left, right):
    return jnp.einsum(spec, left, right, preferred_element_type=f32)


def to_shard(values, mask):
    return lax.ppermute(values, "shard", [(i, i ^ mask) for i in range(4)])


def to_replica(values, mask):
    return lax.ppermute(
        values, "replica", [(i, i ^ mask) for i in range(lax.axis_size("replica"))]
    )


def gather_shards(values):
    pair = jnp.concatenate([values, to_shard(values, 2)], axis=0)
    return jnp.concatenate([pair, to_shard(pair, 1)], axis=0)


def scatter_shards(partial):
    half = partial.shape[0] // 2
    quarter = half // 2
    pair = partial[:half] + to_shard(partial[half:].astype(bf16), 1).astype(f32)
    return pair[:quarter] + to_shard(pair[quarter:].astype(bf16), 2).astype(f32)


def pick(values, index, axis=0):
    return lax.dynamic_index_in_dim(values, index, axis, keepdims=False)


def place_rows(parts, shard_idx):
    rows = parts[0].shape[-2]
    whole = jnp.zeros((*parts[0].shape[:-2], 4 * rows, parts[0].shape[-1]), parts[0].dtype)
    for mask, part in enumerate(parts):
        start = (0,) * (whole.ndim - 2) + ((shard_idx ^ mask) * rows, 0)
        whole = lax.dynamic_update_slice(whole, part, start)
    return whole


def split_columns(shard_idx, parity, gate_weight, up_weight):
    own_rows, columns = gate_weight.shape
    half = columns // 8
    step = 32

    def kernel(who, gate_ref, up_ref, own_a, own_b, near, far_keep, far_pass):
        for odd in range(2):
            for shard in range(4):

                @pl.when((who[0] == shard) & (who[1] == odd))
                def _(odd=odd, shard=shard):
                    kinds = (up_ref, gate_ref) if odd else (gate_ref, up_ref)
                    for h in range(2):

                        def block(kind, mask, h=h):
                            start = (2 * (shard ^ mask) + h) * half
                            return kinds[kind][:, start : start + half]

                        own_a[h] = block(0, 0)
                        own_b[h] = block(1, 0)
                        near[0, h] = block(0, 1)
                        near[1, h] = block(1, 1)
                        far_keep[h] = block(0, 2)
                        far_pass[h] = block(0, 3)

    pair = jax.ShapeDtypeStruct((2, own_rows, half), bf16)
    pair_spec = pl.BlockSpec((2, step, half), lambda i, who: (0, i, 0))
    return pl.pallas_call(
        kernel,
        out_shape=(pair, pair, jax.ShapeDtypeStruct((2, 2, own_rows, half), bf16), pair, pair),
        grid_spec=pltpu.PrefetchScalarGridSpec(
            num_scalar_prefetch=1,
            grid=(own_rows // step,),
            in_specs=[pl.BlockSpec((step, columns), lambda i, who: (i, 0))] * 2,
            out_specs=(
                pair_spec,
                pair_spec,
                pl.BlockSpec((2, 2, step, half), lambda i, who: (0, 0, i, 0)),
                pair_spec,
                pair_spec,
            ),
        ),
        name="split_columns",
    )(jnp.stack([shard_idx, parity]).astype(jnp.int32), gate_weight, up_weight)


def join_rows(shard_idx, own_a, own_b, near, far_a, far_b, near_far):
    _, own_rows, half = own_a.shape

    def kernel(who, own_a, own_b, near, far_a, far_b, near_far, a0, a1, b0, b1):
        outs = ((a0, a1), (b0, b1))
        for mask in range(4):

            @pl.when(pl.program_id(0) == mask)
            def _(mask=mask):
                for kind in range(2):
                    for h in range(2):
                        outs[kind][h][...] = (
                            (own_a, own_b)[kind].at[h],
                            near.at[kind, h],
                            (far_a, far_b)[kind].at[h],
                            near_far.at[kind, h],
                        )[mask][...]

    whole = jax.ShapeDtypeStruct((4 * own_rows, half), bf16)
    pair_spec = pl.BlockSpec((2, own_rows, half), lambda i, who: (0, 0, 0))
    quad_spec = pl.BlockSpec((2, 2, own_rows, half), lambda i, who: (0, 0, 0, 0))
    return pl.pallas_call(
        kernel,
        out_shape=(whole,) * 4,
        grid_spec=pltpu.PrefetchScalarGridSpec(
            num_scalar_prefetch=1,
            grid=(4,),
            in_specs=[pair_spec, pair_spec, quad_spec, pair_spec, pair_spec, quad_spec],
            out_specs=(pl.BlockSpec((own_rows, half), lambda i, who: (who[0] ^ i, 0)),) * 4,
        ),
        name="join_rows",
    )(shard_idx.reshape(1).astype(jnp.int32), own_a, own_b, near, far_a, far_b, near_far)


def reduce_line(pieces, line_idx):
    total = pick(pieces, line_idx).astype(f32)
    for sign in (1, -1):
        moving = None
        for far in (3, 2, 1):
            part = pick(pieces, jnp.clip(line_idx + sign * far, 0, 3)).astype(f32)
            if moving is not None:
                part = part + moving.astype(f32)
            pairs = [
                (i, i + 2 * sign) for i in range(8) if 0 <= i // 2 + sign * far <= 3
            ]
            moving = lax.ppermute(part.astype(bf16), "replica", pairs)
        total = total + moving.astype(f32)
    return total


def shards(
    tokens,
    positions,
    cotangent,
    live_count,
    qkv_weight,
    out_weight,
    gate_weight,
    up_weight,
    down_weight,
    gain_in,
    gain_query,
    gain_key,
    gain_attn,
    gain_pre,
    gain_post,
):
    slot_count, block_len, width = tokens.shape
    rows = slot_count * block_len
    inner = H * HD
    own_rows = gate_weight.shape[0]
    half = gate_weight.shape[1] // 8
    shard_idx = lax.axis_index("shard")
    replica_idx = lax.axis_index("replica")
    parity = replica_idx % 2
    line_idx = replica_idx // 2
    even = parity == 0
    short = lax.axis_size("replica") == 8

    inputs = tokens.reshape(rows, width).astype(f32)
    normed_own = rms_norm(inputs, gain_in).astype(bf16)
    position_own = jnp.broadcast_to(positions.reshape(rows, 1).astype(bf16), (rows, 128))
    gathered_in = gather_shards(jnp.concatenate([normed_own, position_own], axis=1))
    normed_in = gathered_in[:, :width]
    cosine, sine = rotary(gathered_in[:, width].astype(f32))

    def head_of(shard):
        return lax.dynamic_slice_in_dim(qkv_weight, shard * HD, HD, 1)

    kv_own = qkv_weight[:, inner:]
    far_rows = to_shard(
        jnp.concatenate([head_of(shard_idx ^ 2), head_of(shard_idx ^ 3), kv_own], axis=1), 2
    )
    near_rows = to_shard(
        jnp.stack(
            [
                jnp.concatenate([head_of(shard_idx ^ 1), kv_own], axis=1),
                far_rows[:, HD:],
            ]
        ),
        1,
    )
    proj_weight = place_rows(
        [
            jnp.concatenate([head_of(shard_idx), kv_own], axis=1),
            near_rows[0],
            jnp.concatenate([far_rows[:, :HD], far_rows[:, 2 * HD :]], axis=1),
            near_rows[1],
        ],
        shard_idx,
    )

    own_a, own_b, near_mine, keep_mine, pass_mine = split_columns(
        shard_idx, parity, gate_weight, up_weight
    )
    far_pass = to_shard(pass_mine, 2)
    far_keep = to_shard(keep_mine, 2)
    far_pass_b = to_replica(far_pass, 1)
    far_keep_b = to_replica(far_keep, 1)
    near_own = to_shard(near_mine, 1)
    near_far = to_shard(jnp.stack([far_pass, far_pass_b]), 1)
    weights = join_rows(shard_idx, own_a, own_b, near_own, far_keep, far_keep_b, near_far)
    weight_a, weight_b = weights[:2], weights[2:]

    projected = dot("td,df->tf", normed_in, proj_weight)
    query_pre = projected[:, :HD]
    key_pre = projected[:, HD : 2 * HD]
    queries = rotate(rms_norm(query_pre, gain_query), cosine, sine).astype(bf16)
    keys = rotate(rms_norm(key_pre, gain_key), cosine, sine).astype(bf16)
    values = projected[:, 2 * HD :].astype(bf16)
    row_id = jnp.arange(4 * rows, dtype=jnp.int32)
    block_id = row_id // rows
    from_shard = shard_idx ^ ((block_id % 2) * 2 + block_id // 2)
    slot_id = (row_id // block_len) % slot_count
    index = from_shard * block_len + row_id % block_len
    visible = (slot_id[:, None] == slot_id[None, :]) & (index[:, None] >= index[None, :])
    scores = jnp.where(visible, dot("qd,kd->qk", queries, keys) * score_scale, masked_score)
    row_max = jnp.max(scores, axis=-1, keepdims=True)
    log_total = row_max + jnp.log(jnp.sum(jnp.exp(scores - row_max), axis=-1, keepdims=True))
    probs = jnp.exp(scores - log_total)
    probs_bf = probs.astype(bf16)
    mixed = dot("qk,kd->qd", probs_bf, values).astype(bf16)
    attended = scatter_shards(dot("ti,id->td", mixed, out_weight))
    residual = inputs + rms_norm(attended, gain_attn)

    normed_pre = gather_shards(rms_norm(residual, gain_pre).astype(bf16))
    down_halves = [down_weight[:half], down_weight[half:]]
    halves = range(2)
    up_pre, activated, gelu_back, hidden = [None] * 2, [None] * 2, [None] * 2, [None] * 2
    for h in halves:
        pre_a = dot("td,df->tf", normed_pre, weight_a[h])
        pre_b = dot("td,df->tf", normed_pre, weight_b[h])
        up_pre[h] = jnp.where(even, pre_b, pre_a)
        activated[h], gelu_back[h] = jax.vjp(gelu_tanh, jnp.where(even, pre_a, pre_b))
        hidden[h] = (activated[h] * up_pre[h]).astype(bf16)
    ffn_out = scatter_shards(
        dot("tf,fd->td", hidden[0], down_halves[0]) + dot("tf,fd->td", hidden[1], down_halves[1])
    )
    output = residual + rms_norm(ffn_out, gain_post)

    live_slots = (jnp.arange(slot_count, dtype=jnp.int32) < live_count[0]).astype(f32)
    live_rows = jnp.repeat(live_slots, block_len)[:, None]
    upstream = cotangent.reshape(rows, width).astype(f32) * live_rows
    ffn_grad, post_grad = norm_back(ffn_out, gain_post, upstream)
    ffn_grad_bf = gather_shards(ffn_grad.astype(bf16))
    gate_grad_bf, up_grad_bf, pre_part = [None] * 2, [None] * 2, 0.0
    for h in halves:
        hidden_grad = dot("td,fd->tf", ffn_grad_bf, down_halves[h])
        gate_grad_bf[h] = gelu_back[h](hidden_grad * up_pre[h])[0].astype(bf16)
        up_grad_bf[h] = (hidden_grad * activated[h]).astype(bf16)
        grad_a = jnp.where(even, gate_grad_bf[h], up_grad_bf[h])
        grad_b = jnp.where(even, up_grad_bf[h], gate_grad_bf[h])
        pre_part += dot("tf,df->td", grad_a, weight_a[h]) + dot("tf,df->td", grad_b, weight_b[h])
    pre_in_grad = scatter_shards(pre_part)
    res_part, pre_grad = norm_back(residual, gain_pre, pre_in_grad)
    residual_grad = upstream + res_part
    attn_out_grad, attn_grad = norm_back(attended, gain_attn, residual_grad)
    attn_out_bf = gather_shards(attn_out_grad.astype(bf16))

    mixed_grad = dot("td,id->ti", attn_out_bf, out_weight).astype(bf16)
    prob_grad = dot("qd,kd->qk", mixed_grad, values)
    row_dot = jnp.sum(probs * prob_grad, axis=-1, keepdims=True)
    score_grad = (probs * (prob_grad - row_dot) * score_scale).astype(bf16)
    value_part = dot("qk,qd->kd", probs_bf, mixed_grad)
    key_part = dot("qk,qd->kd", score_grad, queries)
    query_grad = dot("qk,kd->qd", score_grad, keys)
    kv_grad = scatter_shards(jnp.concatenate([key_part, value_part], axis=1))
    query_in, query_gain_grad = norm_back(query_pre, gain_query, rotate(query_grad, cosine, -sine))
    query_in_bf = query_in.astype(bf16)
    key_in, key_gain_grad = norm_back(
        key_pre[:rows], gain_key, rotate(kv_grad[:, :HD], cosine[:rows], -sine[:rows])
    )
    kv_in_bf = jnp.concatenate([key_in, kv_grad[:, HD:]], axis=1).astype(bf16)
    normed_grad = scatter_shards(dot("tf,df->td", query_in_bf, proj_weight[:, :HD])) + dot(
        "tf,df->td", kv_in_bf, proj_weight[:, HD:]
    )
    input_part, in_grad = norm_back(inputs, gain_in, normed_grad)
    input_grad = residual_grad + input_part

    normed_owned = lax.dynamic_slice_in_dim(normed_in, shard_idx * own_rows, own_rows, 1)
    packed_own = jnp.concatenate(
        [query_in_bf, kv_in_bf[:, :HD], kv_in_bf[:, HD:]], axis=0
    )[None]
    packed_all = gather_shards(packed_own)
    kv_all = jnp.concatenate(
        [
            jnp.concatenate(
                [packed_all[j, 4 * rows : 5 * rows], packed_all[j, 5 * rows :]], axis=1
            )
            for j in range(4)
        ],
        axis=0,
    )
    qkv_term = jnp.zeros((inner + 2 * HD, own_rows), f32)
    for j, mask in enumerate(BLOCKS):
        theirs = packed_all[j, : 4 * rows].reshape(4, rows, HD)
        ours = jnp.concatenate(
            [theirs[BLOCKS.index(mask ^ BLOCKS[i])] for i in range(4)], axis=0
        )
        qkv_term = lax.dynamic_update_slice(
            qkv_term, dot("tf,td->fd", ours, normed_owned), ((shard_idx ^ mask) * HD, 0)
        )
    qkv_term = lax.dynamic_update_slice(
        qkv_term, dot("tf,td->fd", kv_all, normed_owned), (inner, 0)
    )
    out_term = dot("td,ti->di", attn_out_bf, mixed)

    gains = jnp.concatenate(
        [in_grad, query_gain_grad, key_gain_grad, attn_grad, pre_grad, post_grad]
    )

    def scattered(term, dim):
        return lax.psum_scatter(
            term.astype(bf16), "replica", scatter_dimension=dim, tiled=True
        ).astype(f32)

    out_out = scattered(out_term, 0).T
    qkv_out = scattered(qkv_term, 0).T

    if short:
        hidden_next = [to_replica(hidden[h], 1) for h in halves]
        pre_pair = to_replica(normed_pre[: 2 * rows], 1)
        pre_next = jnp.concatenate([pre_pair, to_shard(pre_pair, 1)], axis=0)

        ffn_cols = ffn_grad_bf.T.reshape(4, 2, width // 8, 4 * rows)
        ffn_mine = pick(ffn_cols, parity, 1).reshape(width // 2, 4 * rows)
        ffn_next = to_replica(pick(ffn_cols, 1 - parity, 1).reshape(width // 2, 4 * rows), 1)
        down_pieces = jnp.stack(
            [
                (
                    dot("ct,tf->cf", ffn_mine, hidden[h]) + dot("ct,tf->cf", ffn_next, hidden_next[h])
                )
                .astype(bf16)
                .reshape(4, width // 8, half)
                for h in halves
            ],
            axis=1,
        )
        down_sum = reduce_line(down_pieces, line_idx)
        down_out = down_sum.transpose(0, 2, 1).reshape(2 * half, width // 8)

        def columns_sum(grad_halves):
            theirs = to_replica(jnp.where(even, grad_halves[1], grad_halves[0]), 1)
            pair = (
                dot("td,tf->df", normed_pre, jnp.where(even, grad_halves[0], grad_halves[1]))
                + dot("td,tf->df", pre_next, theirs)
            ).astype(bf16)
            pair = with_layout_constraint(pair, Layout((0, 1)))

            def rows_of(shard):
                return lax.dynamic_slice_in_dim(pair, shard * own_rows, own_rows, 0)

            pieces = jnp.zeros((4, own_rows, half), bf16)
            pieces = lax.dynamic_update_slice(pieces, rows_of(shard_idx)[None], (shard_idx, 0, 0))
            for mask in (2, 3, 1):
                piece = to_shard(rows_of(shard_idx ^ mask), mask)
                pieces = lax.dynamic_update_slice(pieces, piece[None], (shard_idx ^ mask, 0, 0))
            return reduce_line(pieces, line_idx)

        gate_out = columns_sum(gate_grad_bf)
        up_out = columns_sum(up_grad_bf)
        for mask in (2, 1):
            gains = gains + to_shard(gains, mask)
        for mask in (1, 2, 4):
            gains = gains + to_replica(gains, mask)
    else:
        def columns_sum(grad_halves):
            whole = jnp.concatenate(grad_halves, axis=1)
            pair = dot("td,tf->df", normed_pre, whole).astype(bf16)
            owned = lax.all_to_all(pair, "shard", 0, 1, tiled=True)
            return scattered(owned, 1)

        down_term = dot("tf,tc->fc", jnp.concatenate(hidden, axis=1), ffn_grad_bf)
        down_out = scattered(down_term, 1)
        gate_out = columns_sum(gate_grad_bf)
        up_out = columns_sum(up_grad_bf)
        gains = lax.psum(gains, ("replica", "shard"))

    cuts = [width, width + HD, width + 2 * HD, 2 * width + 2 * HD, 3 * width + 2 * HD]
    return (
        output.reshape(slot_count, block_len, width),
        input_grad.reshape(slot_count, block_len, width),
        qkv_out,
        out_out,
        gate_out,
        up_out,
        down_out,
        *jnp.split(gains, cuts),
    )


def solution(mesh):
    in_specs = (
        P("replica", "shard", None),
        P("replica", "shard"),
        P("replica", "shard", None),
        P("replica"),
        P("shard", None),
        P("shard", None),
        P("shard", None),
        P("shard", None),
        P("shard", None),
        P(),
        P(),
        P(),
        P(),
        P(),
        P(),
    )
    out_specs = (
        P("replica", "shard", None),
        P("replica", "shard", None),
        P("shard", "replica"),
        P("shard", "replica"),
        P("shard", "replica"),
        P("shard", "replica"),
        P("shard", "replica"),
        P(),
        P(),
        P(),
        P(),
        P(),
        P(),
    )
    return jax.shard_map(shards, mesh=mesh, in_specs=in_specs, out_specs=out_specs, check_vma=False)
```
